256 devices in a mesh: ctx: 64 (over z, x_hi, y), tp: 4 (over x_lo, core).
Axes of the slice: x: 4 (x_hi: 2, x_lo: 2; x = x_hi * 2 + x_lo), y: 4, z: 8, core: 2. Of those that a mesh axis runs over, the one named last changes fastest.
Arguments:
- query_raw: bfloat16 [32768, 2048], P('ctx', 'tp'), may hold values from -6 to 6
- key_unnormed: bfloat16 [32768, 1024], P('ctx', 'tp'), may hold values from -6 to 6
- value_matrix: bfloat16 [32768, 1024], P('ctx', 'tp'), may hold values from -6 to 6
- output_grad: bfloat16 [32768, 3840], P(('ctx', 'tp')), may hold values from -24 to 24
- output_weight: bfloat16 [3840, 2048], P('ctx', 'tp'), may hold values from -0.125 to 0.125
Outputs:
- query_grad: bfloat16 [32768, 2048], P('ctx', 'tp')
- key_raw_gradient: bfloat16 [32768, 1024], P('ctx', 'tp')
- value_rows_gradient: bfloat16 [32768, 1024], P('ctx', 'tp')
- weight_grad: float32 [3840, 2048], P('ctx', 'tp')
The draws below stay inside these ranges and needn't reach their ends.
All inputs are finite; a program needn't handle non-finite values.
Results may differ from the reference program's by a relative error of at most 0.01.
Values may be sent and summed in bfloat16 or wider, within the bound.
No kernel may reach another device: no remote copies, remote signals or barrier semaphores. Data moves between devices by JAX's collectives and lax.ppermute only.
A program may use at most 128 MiB of HBM per device.

```python
import jax
import jax.numpy as jnp
from jax import lax

D = 3840
QUERY_HEADS = 8
KEY_VALUE_HEADS = 4
HEAD_SIZE = 256
WINDOW_TOKENS = 1024
SPAN = 512
DOCUMENT_TOKENS = 32768


def strengthened(entries, rng, source, target, blocks, factor):
    def block_of(dim):
        return (jnp.arange(entries.shape[dim]) // (entries.shape[dim] // blocks)).reshape((-1,) + (1,) * (entries.ndim - 1 - dim))

    first = jax.random.permutation(rng, blocks)[block_of(target)]
    second = (block_of(target) + blocks // 2) % blocks
    return jnp.where((block_of(source) == first) | (block_of(source) == second), factor * entries, entries)


def block_levels(stream_key, shape, cuts, smallest, top_value):
    level = 1.0
    for position, parts in cuts:
        steps = jax.random.uniform(jax.random.fold_in(jax.random.fold_in(stream_key, 6), position), (parts,), jnp.float32, smallest / len(cuts), top_value / len(cuts))
        level = level * jnp.repeat(jnp.exp(steps), shape[position] // parts).reshape((-1,) + (1,) * (len(shape) - 1 - position))
    return level


def normal_values(key, extent, width, reach, shards=(), held_as=jnp.bfloat16):
    loudness = block_levels(key, extent, shards, -0.22, 0.18) if shards else 1.0
    values = jax.random.normal(key, extent, jnp.float32) * width * loudness
    return jnp.minimum(jnp.maximum(values, -reach), reach).astype(held_as)


def gaussian_with(own_key, extent, deviation, bound, pieces, heavy, kind=jnp.bfloat16):
    drawn = deviation * jax.random.normal(own_key, extent, jnp.float32)
    if pieces:
        drawn = drawn * block_levels(own_key, extent, pieces, -0.22, 0.18)
    return jnp.clip(strengthened(drawn, jax.random.fold_in(own_key, 3), *heavy), -bound, bound).astype(kind)


def setup_inputs(seed: int = 0) -> dict:
    splits = jax.random.split(jax.random.key(seed), 6)
    query_raw = normal_values(splits[0], (DOCUMENT_TOKENS, QUERY_HEADS * HEAD_SIZE), 1.0, 6.0, ((0, 64), (1, 4)))
    key_unnormed = normal_values(splits[1], (DOCUMENT_TOKENS, KEY_VALUE_HEADS * HEAD_SIZE), 1.0, 6.0, ((0, 64), (1, 4)))
    value_matrix = normal_values(splits[2], (DOCUMENT_TOKENS, KEY_VALUE_HEADS * HEAD_SIZE), 1.0, 6.0, ((0, 64), (1, 4)))
    output_grad = gaussian_with(splits[3], (DOCUMENT_TOKENS, D), 1.0, 24.0, ((0, 256),), (0, 1, 256, 6.0))
    output_weight = normal_values(splits[4], (D, QUERY_HEADS * HEAD_SIZE), (QUERY_HEADS * HEAD_SIZE) ** -0.5, 0.125, ((0, 64), (1, 4)))
    return {"query_raw": query_raw, "key_unnormed": key_unnormed, "value_matrix": value_matrix, "output_grad": output_grad, "output_weight": output_weight}


EPSILON = 1e-06

def normalized_rows(raw, heads):
    token_total = raw.shape[0]
    widened = raw.astype(jnp.float32).reshape(token_total, heads, -1)
    factor = lax.rsqrt(lax.optimization_barrier(jnp.mean(widened * widened, axis=-1, keepdims=True)) + EPSILON)
    return (widened * factor, factor)

def normalized_backward(grad, normed, factor):
    return factor * (grad - normed * lax.optimization_barrier(jnp.mean(grad * normed, axis=-1, keepdims=True)))

def round_low(array):
    return lax.optimization_barrier(array.astype(jnp.bfloat16)).astype(jnp.float32)

def reference(query_raw, key_unnormed, value_matrix, output_grad, output_weight):
    token_total = query_raw.shape[0]
    query_group = QUERY_HEADS // KEY_VALUE_HEADS
    scale = HEAD_SIZE ** (-0.5)
    key_total = WINDOW_TOKENS + SPAN
    q_unit, q_factor = normalized_rows(query_raw, QUERY_HEADS)
    key_normalized, key_factor = normalized_rows(key_unnormed, KEY_VALUE_HEADS)
    q_norm = q_unit.astype(jnp.bfloat16)
    k_norm = key_normalized.astype(jnp.bfloat16)
    value_heads = value_matrix.reshape(token_total, KEY_VALUE_HEADS, HEAD_SIZE)
    grad_heads = jnp.dot(output_grad, output_weight, preferred_element_type=jnp.float32).astype(jnp.bfloat16)
    grad_heads = grad_heads.reshape(token_total, QUERY_HEADS, HEAD_SIZE)
    pad_amount = jnp.zeros((WINDOW_TOKENS, KEY_VALUE_HEADS, HEAD_SIZE), jnp.bfloat16)
    k_padded = jnp.concatenate([pad_amount, k_norm], axis=0)
    v_padded = jnp.concatenate([pad_amount, value_heads], axis=0)
    query_index = jnp.arange(SPAN, dtype=jnp.int32)[:, None]
    key_index = jnp.arange(key_total, dtype=jnp.int32)[None, :]
    banded = (key_index > query_index) & (key_index <= query_index + WINDOW_TOKENS)

    def block_step(carry, block_id):
        key_accumulator, value_accumulator = carry
        first = (block_id * SPAN).astype(jnp.int32)
        query_block = lax.dynamic_slice_in_dim(q_norm, first, SPAN, 0).astype(jnp.float32)
        gradient_block = lax.dynamic_slice_in_dim(grad_heads, first, SPAN, 0).astype(jnp.float32)
        k_block = lax.dynamic_slice_in_dim(k_padded, first, key_total, 0)
        v_block = lax.dynamic_slice_in_dim(v_padded, first, key_total, 0)
        k_wide = jnp.repeat(k_block, query_group, axis=1).astype(jnp.float32)
        v_wide = jnp.repeat(v_block, query_group, axis=1).astype(jnp.float32)
        visible = banded & (first - WINDOW_TOKENS + key_index >= 0)
        scores = jnp.einsum('qhd,khd->hqk', query_block, k_wide) * scale
        weights_exp = jnp.where(visible[None], jnp.exp(scores), 0.0)
        prob = weights_exp / lax.optimization_barrier(jnp.sum(weights_exp, axis=-1, keepdims=True))
        prob_reduced = round_low(prob)
        attended = round_low(jnp.einsum('hqk,khd->qhd', prob_reduced, v_wide))
        delta = lax.optimization_barrier(jnp.sum(gradient_block * attended, axis=-1))
        grad_prob = jnp.einsum('qhd,khd->hqk', gradient_block, v_wide)
        score_gradient = round_low(prob * (grad_prob - jnp.transpose(delta)[:, :, None]) * scale)
        q_grad = jnp.einsum('hqk,khd->qhd', score_gradient, k_wide)
        key_portion = jnp.einsum('juc,ujt->cjt', score_gradient, query_block).reshape(key_total, KEY_VALUE_HEADS, query_group, HEAD_SIZE).sum(axis=2)
        value_portion = jnp.einsum('juc,ujt->cjt', prob_reduced, gradient_block).reshape(key_total, KEY_VALUE_HEADS, query_group, HEAD_SIZE).sum(axis=2)
        key_accumulator = lax.dynamic_update_slice_in_dim(key_accumulator, lax.dynamic_slice_in_dim(key_accumulator, first, key_total, 0) + key_portion, first, 0)
        value_accumulator = lax.dynamic_update_slice_in_dim(value_accumulator, lax.dynamic_slice_in_dim(value_accumulator, first, key_total, 0) + value_portion, first, 0)
        return ((key_accumulator, value_accumulator), (q_grad, attended))
    empty_accumulator = jnp.zeros((WINDOW_TOKENS + token_total, KEY_VALUE_HEADS, HEAD_SIZE), jnp.float32)
    block_ids = jnp.arange(token_total // SPAN, dtype=jnp.int32)
    (key_accumulator, value_accumulator), (q_grads, attended_all) = lax.scan(block_step, (empty_accumulator, empty_accumulator), block_ids)
    q_grads = q_grads.reshape(token_total, QUERY_HEADS, HEAD_SIZE)
    attended_all = attended_all.reshape(token_total, QUERY_HEADS * HEAD_SIZE).astype(jnp.bfloat16)
    weight_grad = jnp.dot(jnp.transpose(output_grad), attended_all, preferred_element_type=jnp.float32)
    query_grad = normalized_backward(q_grads, q_unit, q_factor).astype(jnp.bfloat16).reshape(token_total, QUERY_HEADS * HEAD_SIZE)
    key_raw_gradient = normalized_backward(key_accumulator[WINDOW_TOKENS:], key_normalized, key_factor).astype(jnp.bfloat16).reshape(token_total, KEY_VALUE_HEADS * HEAD_SIZE)
    value_rows_gradient = value_accumulator[WINDOW_TOKENS:].astype(jnp.bfloat16).reshape(token_total, KEY_VALUE_HEADS * HEAD_SIZE)
    return (query_grad, key_raw_gradient, value_rows_gradient, weight_grad)
```

```python
import jax
import jax.numpy as jnp
from jax import lax
from jax.sharding import Mesh, PartitionSpec as P

HEAD_SIZE = 256
WINDOW_TOKENS = 1024
EPSILON = 1e-06
SIZES = {"z": 8, "xh": 2, "y": 4, "xl": 2, "core": 2}
CTX = ("z", "xh", "y")
TP = ("xl", "core")
F32 = jnp.float32
BF16 = jnp.bfloat16


def shift(block, axis, distance):
    size = SIZES[axis]
    return lax.ppermute(block, axis, [(i, (i + distance) % size) for i in range(size)])


def from_behind(block, distance):
    devices = range(SIZES["z"] * SIZES["xh"] * SIZES["y"])
    route = [(i - distance, i) for i in devices if i - distance in devices]
    return lax.ppermute(block, CTX, route)


def normalized_rows(raw, heads):
    token_total = raw.shape[0]
    widened = raw.astype(F32).reshape(token_total, heads, -1)
    factor = lax.rsqrt(jnp.mean(widened * widened, axis=-1, keepdims=True) + EPSILON)
    return (widened * factor, factor)


def normalized_backward(grad, normed, factor):
    return factor * (grad - normed * jnp.mean(grad * normed, axis=-1, keepdims=True))


def contract_last(left, right):
    return lax.dot_general(left, right, (((1,), (1,)), ((), ())), preferred_element_type=F32)


def contract_first(left, right):
    return lax.dot_general(left, right, (((0,), (0,)), ((), ())), preferred_element_type=F32)


def band_mask(query_count, key_total):
    query_index = lax.broadcasted_iota(jnp.int32, (query_count, key_total), 0)
    key_index = lax.broadcasted_iota(jnp.int32, (query_count, key_total), 1)
    return (key_index > query_index) & (key_index <= query_index + WINDOW_TOKENS)


def head_cols(array, index):
    return array[:, index * HEAD_SIZE : (index + 1) * HEAD_SIZE]


def gather_tp(block):
    xl, core = lax.axis_index("xl"), lax.axis_index("core")
    other = shift(block, "xl", 1)
    pair = jnp.where(xl == 0, jnp.stack([block, other]), jnp.stack([other, block]))
    pair_other = shift(pair, "core", 1)
    both = jnp.where(core == 0, jnp.stack([pair, pair_other], 1), jnp.stack([pair_other, pair], 1))
    return both.reshape(4 * block.shape[0], block.shape[1])


def gather_weight(rows):
    y, xh, z = lax.axis_index("y"), lax.axis_index("xh"), lax.axis_index("z")
    w = rows[None]
    far = lax.ppermute(w, "y", [(i, i ^ 1) for i in range(4)])
    w = jnp.where(y % 2 == 0, jnp.concatenate([w, far]), jnp.concatenate([far, w]))
    far = lax.ppermute(w, "y", [(i, i ^ 2) for i in range(4)])
    w = jnp.where(y // 2 == 0, jnp.concatenate([w, far]), jnp.concatenate([far, w]))
    far = shift(w, "xh", 1)
    w = jnp.where(xh == 0, jnp.concatenate([w, far]), jnp.concatenate([far, w]))
    piece = w.reshape(8 * rows.shape[0], -1)
    high = piece.shape[0]
    whole = jnp.zeros((8 * high, piece.shape[1]), piece.dtype)

    def put(whole, part, index):
        return lax.dynamic_update_slice_in_dim(whole, part, (index % 8) * high, 0)

    whole = put(whole, piece, z)
    up = down = piece
    for step in range(1, 5):
        up = shift(up, "z", 1)
        if step < 4:
            down = shift(down, "z", -1)
        whole = put(whole, up, z - step + 8)
        if step < 4:
            whole = put(whole, down, z + step)
    return whole


def scatter_z(total):
    high = total.shape[0] // 8
    z = lax.axis_index("z")

    def own(k):
        return lax.dynamic_slice_in_dim(total, ((z + k + 8) % 8) * high, high, 0)

    up, down = own(3).astype(BF16), own(-4).astype(BF16)
    for k in (2, 1):
        down, up = shift(down, "z", -1), shift(up, "z", 1)
        down = (down.astype(F32) + own(-k - 1)).astype(BF16)
        up = (up.astype(F32) + own(k)).astype(BF16)
    down, up = shift(down, "z", -1), shift(up, "z", 1)
    down = (down.astype(F32) + own(-1)).astype(BF16)
    part = up.astype(F32) + own(0)
    return shift(down, "z", -1).astype(F32) + part


def scatter_xh(pieces, axis):
    xh = lax.axis_index("xh")
    sent = lax.dynamic_index_in_dim(pieces, 1 - xh, axis, keepdims=False).astype(BF16)
    return lax.dynamic_index_in_dim(pieces, xh, axis, keepdims=False) + shift(sent, "xh", 1).astype(F32)


def scatter_y(pieces):
    y = lax.axis_index("y")

    def own(k):
        return lax.dynamic_index_in_dim(pieces, (y + k) % 4, 0, keepdims=False)

    got = [shift(own(k).astype(BF16), "y", k).astype(F32) for k in (1, 2, 3)]
    return own(0) + got[0] + got[1] + got[2]


def scatter_weight_grad(left, right):
    rows = left.shape[0] // 64
    right = scatter_xh(right.reshape(8, 2, 4 * rows, -1), 1).reshape(32 * rows, -1)
    left = scatter_z(left)
    left = scatter_xh(left.reshape(2, 4 * rows, -1), 0)
    right = scatter_z(right)
    return scatter_y(jnp.concatenate([left, right], 1).reshape(4, rows, -1))


def body(query_raw, key_unnormed, value_matrix, output_grad, output_weight):
    block_rows = query_raw.shape[0]
    q_heads = query_raw.shape[1] // HEAD_SIZE
    reach_hops = WINDOW_TOKENS // block_rows
    scale = HEAD_SIZE ** (-0.5)
    q_unit, q_factor = normalized_rows(query_raw, q_heads)
    key_normalized, key_factor = normalized_rows(key_unnormed, 1)
    q_norm = q_unit.astype(BF16).reshape(block_rows, -1)
    k_norm = key_normalized.astype(BF16).reshape(block_rows, -1)
    own_keys = jnp.concatenate([k_norm, value_matrix], axis=1)
    earlier = [from_behind(own_keys, distance) for distance in range(reach_hops, 0, -1)]
    key_rows = jnp.concatenate(earlier + [own_keys], axis=0)
    key_total = key_rows.shape[0]
    keys_all = key_rows[:, :HEAD_SIZE]
    values_all = key_rows[:, HEAD_SIZE:]
    first_key = lax.axis_index(CTX) * block_rows - WINDOW_TOKENS
    key_position = lax.broadcasted_iota(jnp.int32, (block_rows, key_total), 1) + first_key
    visible = band_mask(block_rows, key_total) & (key_position >= 0)
    grad_full = gather_tp(output_grad)
    weight_full = gather_weight(output_weight)
    probs, probs_low, attended = [], [], []
    for h in range(q_heads):
        scores = contract_last(head_cols(q_norm, h), keys_all) * scale
        weights_exp = jnp.where(visible, jnp.exp(scores), 0.0)
        row_total = jnp.sum(weights_exp, axis=1, keepdims=True)
        prob = weights_exp / row_total
        low = prob.astype(BF16)
        attended.append(jnp.dot(low, values_all, preferred_element_type=F32).astype(BF16))
        probs.append(prob)
        probs_low.append(low)
    weight_grad = scatter_weight_grad(
        contract_first(grad_full, attended[0]), contract_first(grad_full, attended[1])
    )
    grad_heads = jnp.dot(grad_full, weight_full, preferred_element_type=F32).astype(BF16)
    key_part = jnp.zeros((key_total, HEAD_SIZE), F32)
    value_part = jnp.zeros((key_total, HEAD_SIZE), F32)
    query_grads = []
    for h in range(q_heads):
        grad_h = head_cols(grad_heads, h)
        delta = jnp.sum(grad_h.astype(F32) * attended[h].astype(F32), axis=1, keepdims=True)
        grad_prob = contract_last(grad_h, values_all)
        score_gradient = (probs[h] * (grad_prob - delta) * scale).astype(BF16)
        query_grads.append(jnp.dot(score_gradient, keys_all, preferred_element_type=F32))
        key_part = key_part + contract_first(score_gradient, head_cols(q_norm, h))
        value_part = value_part + contract_first(probs_low[h], grad_h)
    key_grads = jnp.concatenate([key_part, value_part], axis=1)
    combined = key_grads[WINDOW_TOKENS:]
    for distance in range(1, reach_hops + 1):
        lower = (reach_hops - distance) * block_rows
        combined = combined + from_behind(
            key_grads[lower : lower + block_rows].astype(BF16), -distance
        ).astype(F32)
    q_grad_unit = jnp.concatenate(query_grads, axis=1).reshape(block_rows, q_heads, HEAD_SIZE)
    query_grad = (
        normalized_backward(q_grad_unit, q_unit, q_factor).astype(BF16).reshape(block_rows, -1)
    )
    k_grad_unit = combined[:, :HEAD_SIZE].reshape(block_rows, 1, HEAD_SIZE)
    key_raw_gradient = (
        normalized_backward(k_grad_unit, key_normalized, key_factor)
        .astype(BF16)
        .reshape(block_rows, -1)
    )
    value_rows_gradient = combined[:, HEAD_SIZE:].astype(BF16)
    return (query_grad, key_raw_gradient, value_rows_gradient, weight_grad)


def solution(mesh):
    fine = Mesh(mesh.devices.reshape(tuple(SIZES.values())), tuple(SIZES))
    split = P(CTX, TP)
    placed = (split, split, split, P(CTX + TP, None), split)
    return jax.shard_map(
        body, mesh=fine, in_specs=placed, out_specs=(split,) * 4, check_vma=False
    )
```

```python
import functools

import jax
import jax.numpy as jnp
from jax import lax
from jax.experimental import pallas as pl
from jax.experimental.pallas import tpu as pltpu
from jax.sharding import Mesh, PartitionSpec as P

HEAD_SIZE = 256
WINDOW_TOKENS = 1024
EPSILON = 1e-06
SIZES = {"z": 8, "xh": 2, "y": 4, "xl": 2, "core": 2}
CTX = ("z", "xh", "y")
TP = ("xl", "core")
F32 = jnp.float32
BF16 = jnp.bfloat16
SPAN = 512
CHUNK = 128
REACH = CHUNK + WINDOW_TOKENS
HEADS = 2
SCALE = HEAD_SIZE ** (-0.5)
ANY = pl.BlockSpec(memory_space=pl.ANY)
VMEM = pl.BlockSpec(memory_space=pltpu.VMEM)
SMEM = pl.BlockSpec(memory_space=pltpu.SMEM)


def params(micros):
    return dict(
        compiler_params=pltpu.CompilerParams(vmem_limit_bytes=48 * 2**20),
        cost_estimate=pl.CostEstimate(flops=micros * 10**9, bytes_accessed=2**20, transcendentals=0),
    )


def after(values, *others):
    return lax.optimization_barrier((values, others))[0]


def shift(block, axis, distance):
    size = SIZES[axis]
    return lax.ppermute(block, axis, [(i, (i + distance) % size) for i in range(size)])


def from_behind(block, distance):
    devices = range(SIZES["z"] * SIZES["xh"] * SIZES["y"])
    route = [(i - distance, i) for i in devices if i - distance in devices]
    return lax.ppermute(block, CTX, route)


def normalized_rows(raw):
    widened = raw.astype(F32)
    factor = lax.rsqrt(jnp.mean(widened * widened, axis=-1, keepdims=True) + EPSILON)
    return (widened * factor, factor)


def normalized_backward(grad, normed, factor):
    return factor * (grad - normed * jnp.mean(grad * normed, axis=-1, keepdims=True))


def contract(left, right, left_axis, right_axis):
    return lax.dot_general(
        left, right, (((left_axis,), (right_axis,)), ((), ())), preferred_element_type=F32
    )


def copy_all(pairs, sems):
    copies = [
        pltpu.make_async_copy(source, target, sems.at[i]) for i, (source, target) in enumerate(pairs)
    ]
    for copy in copies:
        copy.start()
    return copies


def chunk_probs(q, k, first_valid, i):
    scores = contract(q, k, 1, 1) * SCALE
    row = lax.broadcasted_iota(jnp.int32, (CHUNK, 1), 0)
    column = lax.broadcasted_iota(jnp.int32, (CHUNK, REACH), 1)
    low = jnp.maximum(row, first_valid - 1 - CHUNK * i)
    visible = (column > low) & (column <= row + WINDOW_TOKENS)
    weights = jnp.where(visible, jnp.exp(scores), 0.0)
    return weights / jnp.sum(weights, axis=1, keepdims=True)


def query_kernel(q_ref, low_ref):
    for h in range(HEADS):
        columns = slice(h * HEAD_SIZE, (h + 1) * HEAD_SIZE)
        unit, _ = normalized_rows(q_ref[:, columns])
        low_ref[:, columns] = unit.astype(BF16)


def norm_queries(query_raw):
    return pl.pallas_call(
        query_kernel,
        out_shape=jax.ShapeDtypeStruct(query_raw.shape, BF16),
        in_specs=[VMEM],
        out_specs=VMEM,
        **params(60),
    )(query_raw)


def query_grad_kernel(grad_ref, q_ref, out_ref):
    for h in range(HEADS):
        columns = slice(h * HEAD_SIZE, (h + 1) * HEAD_SIZE)
        unit, factor = normalized_rows(q_ref[:, columns])
        out_ref[:, columns] = normalized_backward(grad_ref[:, columns], unit, factor).astype(BF16)


def finish_queries(grad, query_raw):
    return pl.pallas_call(
        query_grad_kernel,
        out_shape=jax.ShapeDtypeStruct(query_raw.shape, BF16),
        in_specs=[VMEM, VMEM],
        out_specs=VMEM,
        **params(40),
    )(grad, query_raw)


def forward_kernel(place, q_ref, kv2, kv1, kv0, out_ref, keys, sems):
    copies = copy_all([(ref, keys.at[pl.ds(SPAN * n, SPAN)]) for n, ref in enumerate((kv2, kv1, kv0))], sems)
    first_valid = WINDOW_TOKENS - SPAN * place[0]
    for copy in copies:
        copy.wait()
    for i in range(SPAN // CHUNK):
        rows = slice(CHUNK * i, CHUNK * (i + 1))
        k = keys[CHUNK * i : CHUNK * i + REACH, :HEAD_SIZE]
        v = keys[CHUNK * i : CHUNK * i + REACH, HEAD_SIZE:]
        for h in range(HEADS):
            prob = chunk_probs(q_ref[rows, h * HEAD_SIZE : (h + 1) * HEAD_SIZE], k, first_valid, i)
            out_ref[rows, h * HEAD_SIZE : (h + 1) * HEAD_SIZE] = contract(
                prob.astype(BF16), v, 1, 0
            ).astype(BF16)


def attend(place, query_raw, kv2, kv1, kv0):
    return pl.pallas_call(
        forward_kernel,
        out_shape=jax.ShapeDtypeStruct((SPAN, HEADS * HEAD_SIZE), BF16),
        in_specs=[SMEM, VMEM, ANY, ANY, ANY],
        out_specs=VMEM,
        scratch_shapes=[
            pltpu.VMEM((3 * SPAN, 2 * HEAD_SIZE), BF16),
            pltpu.SemaphoreType.DMA((3,)),
        ],
        **params(15),
    )(place, query_raw, kv2, kv1, kv0)


def grad_rows(place, grads, target):
    xl, core = place[1], place[2]
    size = SPAN // 4
    spots = (xl * 2 + core, (1 - xl) * 2 + core, xl * 2 + 1 - core, (1 - xl) * 2 + 1 - core)
    return [
        (ref, target.at[pl.ds(pl.multiple_of(spot * size, size), size)])
        for ref, spot in zip(grads, spots)
    ]


def weight_kernel(place, att_ref, g0, g1, g2, g3, out_ref, grad, sems):
    copies = copy_all(grad_rows(place, (g0, g1, g2, g3), grad), sems)
    for copy in copies:
        copy.wait()
    tile = HEAD_SIZE
    for n in range(grad.shape[1] // tile):
        part = contract(grad[:, n * tile : (n + 1) * tile], att_ref[...], 0, 0)
        out_ref[n * tile : (n + 1) * tile, :] = part.astype(BF16)


def weight_partials(place, attended, grads):
    width = grads[0].shape[1]
    return pl.pallas_call(
        weight_kernel,
        out_shape=jax.ShapeDtypeStruct((width, HEADS * HEAD_SIZE), BF16),
        in_specs=[SMEM, VMEM] + [ANY] * 4,
        out_specs=VMEM,
        scratch_shapes=[pltpu.VMEM((SPAN, width), BF16), pltpu.SemaphoreType.DMA((4,))],
        **params(20),
    )(place, attended, *grads)


def backward_kernel(pieces, place, q_ref, att_ref, kv2, kv1, kv0, *refs):
    grads, refs = refs[:4], refs[4:]
    parts, refs = refs[:pieces], refs[pieces:]
    query_ref, far_ref, near_ref, own_ref, keys, grad, weight, key_sum, value_sum, sems = refs
    pairs = grad_rows(place, grads, grad) + [(parts[0], weight)]
    pairs += [(ref, keys.at[pl.ds(SPAN * n, SPAN)]) for n, ref in enumerate((kv2, kv1, kv0))]
    copies = copy_all(pairs, sems)
    key_sum[...] = jnp.zeros_like(key_sum)
    value_sum[...] = jnp.zeros_like(value_sum)
    first_valid = WINDOW_TOKENS - SPAN * place[0]
    for copy in copies:
        copy.wait()
    for i in range(SPAN // CHUNK):
        rows = slice(CHUNK * i, CHUNK * (i + 1))
        window = slice(CHUNK * i, CHUNK * i + REACH)
        k, v = keys[window, :HEAD_SIZE], keys[window, HEAD_SIZE:]
        grad_heads = contract(grad[rows, :], weight[...], 1, 0).astype(BF16)
        for h in range(HEADS):
            columns = slice(h * HEAD_SIZE, (h + 1) * HEAD_SIZE)
            q = q_ref[rows, columns]
            grad_h = grad_heads[:, columns]
            prob = chunk_probs(q, k, first_valid, i)
            delta = jnp.sum(
                grad_h.astype(F32) * att_ref[rows, columns].astype(F32), axis=1, keepdims=True
            )
            grad_prob = contract(grad_h, v, 1, 1)
            grad_score = (prob * (grad_prob - delta) * SCALE).astype(BF16)
            query_ref[rows, columns] = contract(grad_score, k, 1, 0)
            key_sum[window, :] += contract(grad_score, q, 0, 0)
            value_sum[window, :] += contract(prob.astype(BF16), grad_h, 0, 0)
    for n, ref in enumerate((far_ref, near_ref, own_ref)):
        rows = slice(SPAN * n, SPAN * (n + 1))
        ref[:, :HEAD_SIZE] = key_sum[rows, :].astype(ref.dtype)
        ref[:, HEAD_SIZE:] = value_sum[rows, :].astype(ref.dtype)


def backward(place, query_raw, attended, keys, grads, parts):
    width = grads[0].shape[1]
    both = 2 * HEAD_SIZE
    return pl.pallas_call(
        functools.partial(backward_kernel, len(parts)),
        out_shape=(
            jax.ShapeDtypeStruct((SPAN, HEADS * HEAD_SIZE), F32),
            jax.ShapeDtypeStruct((SPAN, both), BF16),
            jax.ShapeDtypeStruct((SPAN, both), BF16),
            jax.ShapeDtypeStruct((SPAN, both), F32),
        ),
        in_specs=[SMEM, VMEM, VMEM] + [ANY] * (3 + 4 + len(parts)),
        out_specs=(VMEM,) * 4,
        scratch_shapes=[
            pltpu.VMEM((3 * SPAN, both), BF16),
            pltpu.VMEM((SPAN, width), BF16),
            pltpu.VMEM((width, HEADS * HEAD_SIZE), BF16),
            pltpu.VMEM((3 * SPAN, HEAD_SIZE), F32),
            pltpu.VMEM((3 * SPAN, HEAD_SIZE), F32),
            pltpu.SemaphoreType.DMA((3 + 4 + len(parts),)),
        ],
        **params(25),
    )(place, query_raw, attended, *keys, *grads, *parts)


def gather_y(rows):
    y = lax.axis_index("y")
    w = rows[None]
    far = lax.ppermute(w, "y", [(i, i ^ 1) for i in range(4)])
    w = jnp.where(y % 2 == 0, jnp.concatenate([w, far]), jnp.concatenate([far, w]))
    far = lax.ppermute(w, "y", [(i, i ^ 2) for i in range(4)])
    w = jnp.where(y // 2 == 0, jnp.concatenate([w, far]), jnp.concatenate([far, w]))
    return w.reshape(4 * rows.shape[0], -1)


def scatter(pieces, axes):
    got = lax.all_to_all(pieces.astype(BF16), axes, 0, 0)
    return jnp.sum(got.astype(F32), axis=0)


def body(query_raw, key_unnormed, value_matrix, output_grad, output_weight):
    rows = output_weight.shape[0]
    xh = lax.axis_index("xh")
    place = jnp.stack(
        [lax.axis_index(CTX), lax.axis_index("xl"), lax.axis_index("core"), lax.axis_index("z")]
    ).astype(jnp.int32)
    key_unit, key_factor = normalized_rows(key_unnormed)
    own_keys = jnp.concatenate([key_unit.astype(BF16), value_matrix], axis=1)

    near = gather_y(output_weight)
    across = shift(near, "xh", 1)
    piece = jnp.where(xh == 0, jnp.concatenate([near, across]), jnp.concatenate([across, near]))
    own_keys, xl_source, query_raw, piece = after((own_keys, output_grad, query_raw, piece), piece)
    keys = [from_behind(own_keys, 2), from_behind(own_keys, 1), own_keys]
    xl_grad = shift(xl_source, "xl", 1)
    core_grad = shift(xl_source, "core", 1)
    weight = lax.all_gather(piece, "z", axis=0, tiled=True)
    q_norm = norm_queries(query_raw)
    core_xl_grad = shift(xl_grad, "core", 1)
    attended = attend(place, q_norm, *keys)
    grads = [output_grad, xl_grad, core_grad, core_xl_grad]
    partial = weight_partials(place, attended, grads)
    weight, q_norm = after((weight, q_norm), partial)
    partial = lax.psum_scatter(partial, "z", scatter_dimension=0, tiled=True)
    query_sum, far, close, own = backward(
        place, q_norm, attended, keys, grads, [weight]
    )
    far_got, close_got = from_behind(far, -2), from_behind(close, -1)
    query_grad = finish_queries(query_sum, query_raw)
    weight_grad = scatter(partial.reshape(8, rows, -1), ("xh", "y"))
    combined = own + close_got.astype(F32) + far_got.astype(F32)
    key_raw_gradient = normalized_backward(combined[:, :HEAD_SIZE], key_unit, key_factor).astype(BF16)
    value_rows_gradient = combined[:, HEAD_SIZE:].astype(BF16)
    return (query_grad, key_raw_gradient, value_rows_gradient, weight_grad)


def solution(mesh):
    fine = Mesh(mesh.devices.reshape(tuple(SIZES.values())), tuple(SIZES))
    split = P(CTX, TP)
    placed = (split, split, split, P(CTX + TP, None), split)
    return jax.shard_map(
        body, mesh=fine, in_specs=placed, out_specs=(split,) * 4, check_vma=False
    )
```

```python
import functools

import jax
import jax.numpy as jnp
from jax import lax
from jax.experimental import pallas as pl
from jax.experimental.pallas import tpu as pltpu
from jax.sharding import Mesh, PartitionSpec as P

HEAD_SIZE = 256
WINDOW_TOKENS = 1024
EPSILON = 1e-06
SIZES = {"z": 8, "xh": 2, "y": 4, "xl": 2, "core": 2}
CTX = ("z", "xh", "y")
TP = ("xl", "core")
F32 = jnp.float32
BF16 = jnp.bfloat16
SPAN = 512
CHUNK = 128
REACH = CHUNK + WINDOW_TOKENS
HEADS = 2
SCALE = HEAD_SIZE ** (-0.5)
ANY = pl.BlockSpec(memory_space=pl.ANY)
VMEM = pl.BlockSpec(memory_space=pltpu.VMEM)
SMEM = pl.BlockSpec(memory_space=pltpu.SMEM)


def params(micros):
    return dict(
        compiler_params=pltpu.CompilerParams(vmem_limit_bytes=48 * 2**20),
        cost_estimate=pl.CostEstimate(flops=micros * 10**9, bytes_accessed=2**20, transcendentals=0),
    )


def after(values, *others):
    return lax.optimization_barrier((values, others))[0]


def shift(block, axis, distance):
    size = SIZES[axis]
    return lax.ppermute(block, axis, [(i, (i + distance) % size) for i in range(size)])


def from_behind(block, distance):
    devices = range(SIZES["z"] * SIZES["xh"] * SIZES["y"])
    route = [(i - distance, i) for i in devices if i - distance in devices]
    return lax.ppermute(block, CTX, route)


def normalized_rows(raw):
    widened = raw.astype(F32)
    factor = lax.rsqrt(jnp.mean(widened * widened, axis=-1, keepdims=True) + EPSILON)
    return (widened * factor, factor)


def normalized_backward(grad, normed, factor):
    return factor * (grad - normed * jnp.mean(grad * normed, axis=-1, keepdims=True))


def contract(left, right, left_axis, right_axis):
    return lax.dot_general(
        left, right, (((left_axis,), (right_axis,)), ((), ())), preferred_element_type=F32
    )


def copy_all(pairs, sems):
    copies = [
        pltpu.make_async_copy(source, target, sems.at[i]) for i, (source, target) in enumerate(pairs)
    ]
    for copy in copies:
        copy.start()
    return copies


def chunk_probs(q, k, first_valid, i):
    scores = contract(q, k, 1, 1) * SCALE
    row = lax.broadcasted_iota(jnp.int32, (CHUNK, 1), 0)
    column = lax.broadcasted_iota(jnp.int32, (CHUNK, REACH), 1)
    low = jnp.maximum(row, first_valid - 1 - CHUNK * i)
    visible = (column > low) & (column <= row + WINDOW_TOKENS)
    weights = jnp.where(visible, jnp.exp(scores), 0.0)
    return weights / jnp.sum(weights, axis=1, keepdims=True)


def query_kernel(q_ref, low_ref):
    for h in range(HEADS):
        columns = slice(h * HEAD_SIZE, (h + 1) * HEAD_SIZE)
        unit, _ = normalized_rows(q_ref[:, columns])
        low_ref[:, columns] = unit.astype(BF16)


def norm_queries(query_raw):
    return pl.pallas_call(
        query_kernel,
        out_shape=jax.ShapeDtypeStruct(query_raw.shape, BF16),
        in_specs=[VMEM],
        out_specs=VMEM,
        **params(60),
    )(query_raw)


def query_grad_kernel(grad_ref, q_ref, out_ref):
    for h in range(HEADS):
        columns = slice(h * HEAD_SIZE, (h + 1) * HEAD_SIZE)
        unit, factor = normalized_rows(q_ref[:, columns])
        out_ref[:, columns] = normalized_backward(grad_ref[:, columns], unit, factor).astype(BF16)


def finish_queries(grad, query_raw):
    return pl.pallas_call(
        query_grad_kernel,
        out_shape=jax.ShapeDtypeStruct(query_raw.shape, BF16),
        in_specs=[VMEM, VMEM],
        out_specs=VMEM,
        **params(40),
    )(grad, query_raw)


def forward_kernel(place, q_ref, kv2, kv1, kv0, out_ref, keys, sems):
    copies = copy_all([(ref, keys.at[pl.ds(SPAN * n, SPAN)]) for n, ref in enumerate((kv2, kv1, kv0))], sems)
    first_valid = WINDOW_TOKENS - SPAN * place[0]
    for copy in copies:
        copy.wait()
    for i in range(SPAN // CHUNK):
        rows = slice(CHUNK * i, CHUNK * (i + 1))
        k = keys[CHUNK * i : CHUNK * i + REACH, :HEAD_SIZE]
        v = keys[CHUNK * i : CHUNK * i + REACH, HEAD_SIZE:]
        for h in range(HEADS):
            prob = chunk_probs(q_ref[rows, h * HEAD_SIZE : (h + 1) * HEAD_SIZE], k, first_valid, i)
            out_ref[rows, h * HEAD_SIZE : (h + 1) * HEAD_SIZE] = contract(
                prob.astype(BF16), v, 1, 0
            ).astype(BF16)


def attend(place, query_raw, kv2, kv1, kv0):
    return pl.pallas_call(
        forward_kernel,
        out_shape=jax.ShapeDtypeStruct((SPAN, HEADS * HEAD_SIZE), BF16),
        in_specs=[SMEM, VMEM, ANY, ANY, ANY],
        out_specs=VMEM,
        scratch_shapes=[
            pltpu.VMEM((3 * SPAN, 2 * HEAD_SIZE), BF16),
            pltpu.SemaphoreType.DMA((3,)),
        ],
        **params(15),
    )(place, query_raw, kv2, kv1, kv0)


def grad_rows(place, grads, target):
    xl, core = place[1], place[2]
    size = SPAN // 4
    spots = (xl * 2 + core, (1 - xl) * 2 + core, xl * 2 + 1 - core, (1 - xl) * 2 + 1 - core)
    return [
        (ref, target.at[pl.ds(pl.multiple_of(spot * size, size), size)])
        for ref, spot in zip(grads, spots)
    ]


def weight_kernel(place, att_ref, g0, g1, g2, g3, out_ref, grad, sems):
    copies = copy_all(grad_rows(place, (g0, g1, g2, g3), grad), sems)
    for copy in copies:
        copy.wait()
    tile = HEAD_SIZE
    for n in range(grad.shape[1] // tile):
        part = contract(grad[:, n * tile : (n + 1) * tile], att_ref[...], 0, 0)
        out_ref[n * tile : (n + 1) * tile, :] = part.astype(BF16)


def weight_partials(place, attended, grads):
    width = grads[0].shape[1]
    return pl.pallas_call(
        weight_kernel,
        out_shape=jax.ShapeDtypeStruct((width, HEADS * HEAD_SIZE), BF16),
        in_specs=[SMEM, VMEM] + [ANY] * 4,
        out_specs=VMEM,
        scratch_shapes=[pltpu.VMEM((SPAN, width), BF16), pltpu.SemaphoreType.DMA((4,))],
        **params(20),
    )(place, attended, *grads)


def backward_kernel(pieces, place, q_ref, att_ref, kv2, kv1, kv0, *refs):
    grads, refs = refs[:4], refs[4:]
    parts, refs = refs[:pieces], refs[pieces:]
    query_ref, far_ref, near_ref, own_ref, keys, grad, weight, key_sum, value_sum, sems = refs
    pairs = grad_rows(place, grads, grad) + [(parts[0], weight)]
    pairs += [(ref, keys.at[pl.ds(SPAN * n, SPAN)]) for n, ref in enumerate((kv2, kv1, kv0))]
    copies = copy_all(pairs, sems)
    key_sum[...] = jnp.zeros_like(key_sum)
    value_sum[...] = jnp.zeros_like(value_sum)
    first_valid = WINDOW_TOKENS - SPAN * place[0]
    for copy in copies[-3:]:
        copy.wait()
    probs = [
        [
            chunk_probs(
                q_ref[CHUNK * i : CHUNK * (i + 1), h * HEAD_SIZE : (h + 1) * HEAD_SIZE],
                keys[CHUNK * i : CHUNK * i + REACH, :HEAD_SIZE],
                first_valid,
                i,
            )
            for h in range(HEADS)
        ]
        for i in range(SPAN // CHUNK)
    ]
    for copy in copies[:-3]:
        copy.wait()
    for i in range(SPAN // CHUNK):
        rows = slice(CHUNK * i, CHUNK * (i + 1))
        window = slice(CHUNK * i, CHUNK * i + REACH)
        k, v = keys[window, :HEAD_SIZE], keys[window, HEAD_SIZE:]
        grad_heads = contract(grad[rows, :], weight[...], 1, 0).astype(BF16)
        for h in range(HEADS):
            columns = slice(h * HEAD_SIZE, (h + 1) * HEAD_SIZE)
            q = q_ref[rows, columns]
            grad_h = grad_heads[:, columns]
            prob = probs[i][h]
            delta = jnp.sum(
                grad_h.astype(F32) * att_ref[rows, columns].astype(F32), axis=1, keepdims=True
            )
            grad_prob = contract(grad_h, v, 1, 1)
            grad_score = (prob * (grad_prob - delta) * SCALE).astype(BF16)
            query_ref[rows, columns] = contract(grad_score, k, 1, 0)
            key_sum[window, :] += contract(grad_score, q, 0, 0)
            value_sum[window, :] += contract(prob.astype(BF16), grad_h, 0, 0)
    for n, ref in enumerate((far_ref, near_ref, own_ref)):
        rows = slice(SPAN * n, SPAN * (n + 1))
        ref[:, :HEAD_SIZE] = key_sum[rows, :].astype(ref.dtype)
        ref[:, HEAD_SIZE:] = value_sum[rows, :].astype(ref.dtype)


def backward(place, query_raw, attended, keys, grads, parts):
    width = grads[0].shape[1]
    both = 2 * HEAD_SIZE
    return pl.pallas_call(
        functools.partial(backward_kernel, len(parts)),
        out_shape=(
            jax.ShapeDtypeStruct((SPAN, HEADS * HEAD_SIZE), F32),
            jax.ShapeDtypeStruct((SPAN, both), BF16),
            jax.ShapeDtypeStruct((SPAN, both), BF16),
            jax.ShapeDtypeStruct((SPAN, both), F32),
        ),
        in_specs=[SMEM, VMEM, VMEM] + [ANY] * (3 + 4 + len(parts)),
        out_specs=(VMEM,) * 4,
        scratch_shapes=[
            pltpu.VMEM((3 * SPAN, both), BF16),
            pltpu.VMEM((SPAN, width), BF16),
            pltpu.VMEM((width, HEADS * HEAD_SIZE), BF16),
            pltpu.VMEM((3 * SPAN, HEAD_SIZE), F32),
            pltpu.VMEM((3 * SPAN, HEAD_SIZE), F32),
            pltpu.SemaphoreType.DMA((3 + 4 + len(parts),)),
        ],
        **params(25),
    )(place, query_raw, attended, *keys, *grads, *parts)


def scatter(pieces, axes):
    got = lax.all_to_all(pieces.astype(BF16), axes, 0, 0)
    return jnp.sum(got.astype(F32), axis=0)


def body(query_raw, key_unnormed, value_matrix, output_grad, output_weight):
    rows = output_weight.shape[0]
    xh = lax.axis_index("xh")
    place = jnp.stack(
        [lax.axis_index(CTX), lax.axis_index("xl"), lax.axis_index("core"), lax.axis_index("z")]
    ).astype(jnp.int32)
    key_unit, key_factor = normalized_rows(key_unnormed)
    own_keys = jnp.concatenate([key_unit.astype(BF16), value_matrix], axis=1)

    core_grad = shift(output_grad, "core", 1)
    spread = jnp.broadcast_to(output_weight, (8,) + output_weight.shape)
    piece = lax.all_to_all(spread, ("xh", "y"), 0, 0).reshape(8 * rows, -1)
    core_grad, xl_source, piece = after((core_grad, output_grad, piece), piece, core_grad)
    own_keys, query_raw = after((own_keys, query_raw), piece)
    xl_grad = shift(xl_source, "xl", 1)
    behind = from_behind(own_keys, 1)
    keys = [from_behind(behind, 1), behind, own_keys]
    xl_grad = after(xl_grad, keys[0])
    weight = lax.all_gather(piece, "z", axis=0, tiled=True)
    q_norm = norm_queries(query_raw)
    core_xl_grad = shift(xl_grad, "core", 1)
    attended = attend(place, q_norm, *keys)
    grads = [output_grad, xl_grad, core_grad, core_xl_grad]
    partial = weight_partials(place, attended, grads)
    weight, q_norm = after((weight, q_norm), partial)
    partial = lax.psum_scatter(partial, "z", scatter_dimension=0, tiled=True)
    query_sum, far, close, own = backward(
        place, q_norm, attended, keys, grads, [weight]
    )
    passed_on = from_behind(far, -1).astype(F32) + close.astype(F32)
    passed_on = from_behind(passed_on.astype(BF16), -1)
    query_grad = finish_queries(query_sum, query_raw)
    weight_grad = scatter(partial.reshape(8, rows, -1), ("xh", "y"))
    passed_on = after(passed_on, weight_grad)
    combined = own + passed_on.astype(F32)
    key_raw_gradient = normalized_backward(combined[:, :HEAD_SIZE], key_unit, key_factor).astype(BF16)
    value_rows_gradient = combined[:, HEAD_SIZE:].astype(BF16)
    return (query_grad, key_raw_gradient, value_rows_gradient, weight_grad)


def solution(mesh):
    fine = Mesh(mesh.devices.reshape(tuple(SIZES.values())), tuple(SIZES))
    split = P(CTX, TP)
    placed = (split, split, split, P(CTX + TP, None), split)
    return jax.shard_map(
        body, mesh=fine, in_specs=placed, out_specs=(split,) * 4, check_vma=False
    )
```

```python
import functools

import jax
import jax.numpy as jnp
from jax import lax
from jax.experimental import pallas as pl
from jax.experimental.pallas import tpu as pltpu
from jax.sharding import Mesh, PartitionSpec as P

HEAD_SIZE = 256
WINDOW_TOKENS = 1024
EPSILON = 1e-06
SIZES = {"z": 8, "xh": 2, "y": 4, "xl": 2, "core": 2}
CTX = ("z", "xh", "y")
TP = ("xl", "core")
F32 = jnp.float32
BF16 = jnp.bfloat16
SPAN = 512
CHUNK = 128
REACH = CHUNK + WINDOW_TOKENS
HEADS = 2
SCALE = HEAD_SIZE ** (-0.5)
ANY = pl.BlockSpec(memory_space=pl.ANY)
VMEM = pl.BlockSpec(memory_space=pltpu.VMEM)
SMEM = pl.BlockSpec(memory_space=pltpu.SMEM)


def params(micros):
    return dict(
        compiler_params=pltpu.CompilerParams(vmem_limit_bytes=48 * 2**20),
        cost_estimate=pl.CostEstimate(flops=micros * 10**9, bytes_accessed=2**20, transcendentals=0),
    )


def after(values, *others):
    return lax.optimization_barrier((values, others))[0]


def shift(block, axis, distance):
    size = SIZES[axis]
    return lax.ppermute(block, axis, [(i, (i + distance) % size) for i in range(size)])


def from_behind(block, distance):
    devices = range(SIZES["z"] * SIZES["xh"] * SIZES["y"])
    route = [(i - distance, i) for i in devices if i - distance in devices]
    return lax.ppermute(block, CTX, route)


def normalized_rows(raw):
    widened = raw.astype(F32)
    factor = lax.rsqrt(jnp.mean(widened * widened, axis=-1, keepdims=True) + EPSILON)
    return (widened * factor, factor)


def normalized_backward(grad, normed, factor):
    return factor * (grad - normed * jnp.mean(grad * normed, axis=-1, keepdims=True))


def contract(left, right, left_axis, right_axis):
    return lax.dot_general(
        left, right, (((left_axis,), (right_axis,)), ((), ())), preferred_element_type=F32
    )


def copy_all(pairs, sems):
    copies = [
        pltpu.make_async_copy(source, target, sems.at[i]) for i, (source, target) in enumerate(pairs)
    ]
    for copy in copies:
        copy.start()
    return copies


def chunk_probs(q, k, first_valid, i):
    scores = contract(q, k, 1, 1) * SCALE
    row = lax.broadcasted_iota(jnp.int32, (CHUNK, 1), 0)
    column = lax.broadcasted_iota(jnp.int32, (CHUNK, REACH), 1)
    low = jnp.maximum(row, first_valid - 1 - CHUNK * i)
    visible = (column > low) & (column <= row + WINDOW_TOKENS)
    weights = jnp.where(visible, jnp.exp(scores), 0.0)
    return weights / jnp.sum(weights, axis=1, keepdims=True)


def query_kernel(q_ref, low_ref):
    for h in range(HEADS):
        columns = slice(h * HEAD_SIZE, (h + 1) * HEAD_SIZE)
        unit, _ = normalized_rows(q_ref[:, columns])
        low_ref[:, columns] = unit.astype(BF16)


def norm_queries(query_raw):
    return pl.pallas_call(
        query_kernel,
        out_shape=jax.ShapeDtypeStruct(query_raw.shape, BF16),
        in_specs=[VMEM],
        out_specs=VMEM,
        **params(60),
    )(query_raw)


def query_grad_kernel(grad_ref, q_ref, out_ref):
    for h in range(HEADS):
        columns = slice(h * HEAD_SIZE, (h + 1) * HEAD_SIZE)
        unit, factor = normalized_rows(q_ref[:, columns])
        out_ref[:, columns] = normalized_backward(grad_ref[:, columns], unit, factor).astype(BF16)


def finish_queries(grad, query_raw):
    return pl.pallas_call(
        query_grad_kernel,
        out_shape=jax.ShapeDtypeStruct(query_raw.shape, BF16),
        in_specs=[VMEM, VMEM],
        out_specs=VMEM,
        **params(40),
    )(grad, query_raw)


def forward_kernel(place, q_ref, kv2, kv1, kv0, out_ref, keys, sems):
    copies = copy_all([(ref, keys.at[pl.ds(SPAN * n, SPAN)]) for n, ref in enumerate((kv2, kv1, kv0))], sems)
    first_valid = WINDOW_TOKENS - SPAN * place[0]
    for copy in copies:
        copy.wait()
    for i in range(SPAN // CHUNK):
        rows = slice(CHUNK * i, CHUNK * (i + 1))
        k = keys[CHUNK * i : CHUNK * i + REACH, :HEAD_SIZE]
        v = keys[CHUNK * i : CHUNK * i + REACH, HEAD_SIZE:]
        for h in range(HEADS):
            prob = chunk_probs(q_ref[rows, h * HEAD_SIZE : (h + 1) * HEAD_SIZE], k, first_valid, i)
            out_ref[rows, h * HEAD_SIZE : (h + 1) * HEAD_SIZE] = contract(
                prob.astype(BF16), v, 1, 0
            ).astype(BF16)


def attend(place, query_raw, kv2, kv1, kv0):
    return pl.pallas_call(
        forward_kernel,
        out_shape=jax.ShapeDtypeStruct((SPAN, HEADS * HEAD_SIZE), BF16),
        in_specs=[SMEM, VMEM, ANY, ANY, ANY],
        out_specs=VMEM,
        scratch_shapes=[
            pltpu.VMEM((3 * SPAN, 2 * HEAD_SIZE), BF16),
            pltpu.SemaphoreType.DMA((3,)),
        ],
        **params(15),
    )(place, query_raw, kv2, kv1, kv0)


def grad_rows(place, grads, target):
    xl, core = place[1], place[2]
    size = SPAN // 4
    spots = (xl * 2 + core, (1 - xl) * 2 + core, xl * 2 + 1 - core, (1 - xl) * 2 + 1 - core)
    return [
        (ref, target.at[pl.ds(pl.multiple_of(spot * size, size), size)])
        for ref, spot in zip(grads, spots)
    ]


def weight_kernel(place, att_ref, g0, g1, g2, g3, left_ref, right_ref, grad, right, sems):
    copies = copy_all(grad_rows(place, (g0, g1, g2, g3), grad), sems)
    for copy in copies:
        copy.wait()
    tile = HEAD_SIZE
    for n in range(grad.shape[1] // tile):
        part = contract(grad[:, n * tile : (n + 1) * tile], att_ref[...], 0, 0)
        left_ref[n * tile : (n + 1) * tile, :] = part[:, :HEAD_SIZE].astype(BF16)
        right[n * tile : (n + 1) * tile, :] = part[:, HEAD_SIZE:]
    inner, outer, rows, _ = right_ref.shape
    for n in range(outer):
        for y in range(inner):
            first = (n * inner + y) * rows
            right_ref[y, n] = right[first : first + rows, :].astype(BF16)


def weight_partials(place, attended, grads):
    width = grads[0].shape[1]
    return pl.pallas_call(
        weight_kernel,
        out_shape=(
            jax.ShapeDtypeStruct((width, HEAD_SIZE), BF16),
            jax.ShapeDtypeStruct((4, 16, width // 64, HEAD_SIZE), BF16),
        ),
        in_specs=[SMEM, VMEM] + [ANY] * 4,
        out_specs=(VMEM, VMEM),
        scratch_shapes=[
            pltpu.VMEM((SPAN, width), BF16),
            pltpu.VMEM((width, HEAD_SIZE), F32),
            pltpu.SemaphoreType.DMA((4,)),
        ],
        **params(20),
    )(place, attended, *grads)


def backward_kernel(pieces, place, q_ref, att_ref, kv2, kv1, kv0, *refs):
    grads, refs = refs[:4], refs[4:]
    parts, refs = refs[:pieces], refs[pieces:]
    query_ref, far_ref, near_ref, own_ref, keys, grad, weight, key_sum, value_sum, sems = refs
    pairs = grad_rows(place, grads, grad) + [(parts[0], weight)]
    pairs += [(ref, keys.at[pl.ds(SPAN * n, SPAN)]) for n, ref in enumerate((kv2, kv1, kv0))]
    copies = copy_all(pairs, sems)
    key_sum[...] = jnp.zeros_like(key_sum)
    value_sum[...] = jnp.zeros_like(value_sum)
    first_valid = WINDOW_TOKENS - SPAN * place[0]
    for copy in copies[-3:]:
        copy.wait()
    probs = [
        [
            chunk_probs(
                q_ref[CHUNK * i : CHUNK * (i + 1), h * HEAD_SIZE : (h + 1) * HEAD_SIZE],
                keys[CHUNK * i : CHUNK * i + REACH, :HEAD_SIZE],
                first_valid,
                i,
            )
            for h in range(HEADS)
        ]
        for i in range(SPAN // CHUNK)
    ]
    for copy in copies[:-3]:
        copy.wait()
    for i in range(SPAN // CHUNK):
        rows = slice(CHUNK * i, CHUNK * (i + 1))
        window = slice(CHUNK * i, CHUNK * i + REACH)
        k, v = keys[window, :HEAD_SIZE], keys[window, HEAD_SIZE:]
        grad_heads = contract(grad[rows, :], weight[...], 1, 0).astype(BF16)
        for h in range(HEADS):
            columns = slice(h * HEAD_SIZE, (h + 1) * HEAD_SIZE)
            q = q_ref[rows, columns]
            grad_h = grad_heads[:, columns]
            prob = probs[i][h]
            delta = jnp.sum(
                grad_h.astype(F32) * att_ref[rows, columns].astype(F32), axis=1, keepdims=True
            )
            grad_prob = contract(grad_h, v, 1, 1)
            grad_score = (prob * (grad_prob - delta) * SCALE).astype(BF16)
            query_ref[rows, columns] = contract(grad_score, k, 1, 0)
            key_sum[window, :] += contract(grad_score, q, 0, 0)
            value_sum[window, :] += contract(prob.astype(BF16), grad_h, 0, 0)
    for n, ref in enumerate((far_ref, near_ref, own_ref)):
        rows = slice(SPAN * n, SPAN * (n + 1))
        ref[:, :HEAD_SIZE] = key_sum[rows, :].astype(ref.dtype)
        ref[:, HEAD_SIZE:] = value_sum[rows, :].astype(ref.dtype)


def backward(place, query_raw, attended, keys, grads, parts):
    width = grads[0].shape[1]
    both = 2 * HEAD_SIZE
    return pl.pallas_call(
        functools.partial(backward_kernel, len(parts)),
        out_shape=(
            jax.ShapeDtypeStruct((SPAN, HEADS * HEAD_SIZE), F32),
            jax.ShapeDtypeStruct((SPAN, both), BF16),
            jax.ShapeDtypeStruct((SPAN, both), BF16),
            jax.ShapeDtypeStruct((SPAN, both), F32),
        ),
        in_specs=[SMEM, VMEM, VMEM] + [ANY] * (3 + 4 + len(parts)),
        out_specs=(VMEM,) * 4,
        scratch_shapes=[
            pltpu.VMEM((3 * SPAN, both), BF16),
            pltpu.VMEM((SPAN, width), BF16),
            pltpu.VMEM((width, HEADS * HEAD_SIZE), BF16),
            pltpu.VMEM((3 * SPAN, HEAD_SIZE), F32),
            pltpu.VMEM((3 * SPAN, HEAD_SIZE), F32),
            pltpu.SemaphoreType.DMA((3 + 4 + len(parts),)),
        ],
        **params(25),
    )(place, query_raw, attended, *keys, *grads, *parts)


def scatter(pieces, axes):
    got = lax.all_to_all(pieces.astype(BF16), axes, 0, 0)
    return jnp.sum(got.astype(F32), axis=0)


def body(query_raw, key_unnormed, value_matrix, output_grad, output_weight):
    rows = output_weight.shape[0]
    xh = lax.axis_index("xh")
    place = jnp.stack(
        [lax.axis_index(CTX), lax.axis_index("xl"), lax.axis_index("core"), lax.axis_index("z")]
    ).astype(jnp.int32)
    key_unit, key_factor = normalized_rows(key_unnormed)
    own_keys = jnp.concatenate([key_unit.astype(BF16), value_matrix], axis=1)

    core_grad = shift(output_grad, "core", 1)
    spread = jnp.broadcast_to(output_weight, (8,) + output_weight.shape)
    piece = lax.all_to_all(spread, ("xh", "y"), 0, 0).reshape(8 * rows, -1)
    core_grad, xl_source, piece = after((core_grad, output_grad, piece), piece, core_grad)
    q_norm = norm_queries(after(query_raw, piece))
    own_keys = after(own_keys, q_norm)
    xl_grad = shift(xl_source, "xl", 1)
    keys = [from_behind(own_keys, 2), from_behind(own_keys, 1), own_keys]
    weight = lax.all_gather(piece, "z", axis=0, tiled=True)
    core_xl_grad = shift(xl_grad, "core", 1)
    attended = attend(place, q_norm, *keys)
    grads = [output_grad, xl_grad, core_grad, core_xl_grad]
    left, right = weight_partials(place, attended, grads)
    y = lax.axis_index("y")
    sent = [lax.dynamic_index_in_dim(right, (y + k) % 4, 0, keepdims=False) for k in range(4)]
    got = [shift(sent[k], "y", k) for k in (1, 2, 3)]
    weight, q_norm = after((weight, q_norm), left, sent)
    left = lax.psum_scatter(left, "z", scatter_dimension=0, tiled=True)
    query_sum, far, close, own = backward(
        place, q_norm, attended, keys, grads, [weight]
    )
    far_got, close_got = from_behind(far, -2), from_behind(close, -1)
    query_grad = finish_queries(query_sum, query_raw)
    got = after(got, query_grad)
    right = sum((part.astype(F32) for part in got), sent[0].astype(F32))
    right = scatter(right, ("z", "xh"))
    left = scatter(after(left, right).reshape(8, rows, -1), ("xh", "y"))
    weight_grad = jnp.concatenate([left, right], 1)
    far_got, close_got = after((far_got, close_got), weight_grad)
    combined = own + close_got.astype(F32) + far_got.astype(F32)
    key_raw_gradient = normalized_backward(combined[:, :HEAD_SIZE], key_unit, key_factor).astype(BF16)
    value_rows_gradient = combined[:, HEAD_SIZE:].astype(BF16)
    return (query_grad, key_raw_gradient, value_rows_gradient, weight_grad)


def solution(mesh):
    fine = Mesh(mesh.devices.reshape(tuple(SIZES.values())), tuple(SIZES))
    split = P(CTX, TP)
    placed = (split, split, split, P(CTX + TP, None), split)
    return jax.shard_map(
        body, mesh=fine, in_specs=placed, out_specs=(split,) * 4, check_vma=False
    )
```
